32 devices in a mesh: ka: 4 (over y, x), hist: 8 (over z, core).
Axes of the slice: x: 2, y: 2, z: 4, core: 2. Of those that a mesh axis runs over, the one named last changes fastest.
Arguments:
- step_index: int32 [1], replicated, may hold values from 9 to 32
- band_energy: float32 [32, 3, 512], P('hist', None, 'ka'), may hold values from -1 to 3
- kernel_row: bfloat16 [32, 2, 3, 3, 512], P('hist', None, None, None, 'ka'), may hold values from -0.5 to 0.5
- lattice_history: bfloat16 [32, 2, 3, 3, 32, 512], P('hist', None, None, None, None, 'ka'), may hold values from -6 to 6, as said below
- diagonal_inverse: float32 [2, 3, 3, 512], P(None, None, None, 'ka'), may hold values from -3 to 3
- multiplicity: int32 [512], P('ka'), may hold values from 1 to 32, as said below
- state_energy: float32 [64], replicated, may hold values from -3 to 3
- connection: int32 [64, 6], replicated, may hold values from 0 to 63, as said below
- predicted_row: float32 [2, 64, 32], P(None, None, 'hist'), may hold values from -6 to 6
- pseudo_history: bfloat16 [32, 2, 64, 32], P('hist'), may hold values from -6 to 6, as said below
Outputs:
- lattice_row: bfloat16 [32, 2, 3, 3, 512], P('hist', None, None, None, 'ka')
- local_row: float32 [2, 3, 3, 32], P(None, None, None, 'hist')
- pseudo_row: float32 [2, 64, 32], P(None, None, 'hist')
The draws below stay inside these ranges and needn't reach their ends.
Inputs may be any that keep to these rules, and one draw needn't show every extreme that they name: `lattice_history`: the stored lattice propagators vanish where the column time j exceeds the row time m. `pseudo_history`: the stored pseudo-particle propagators vanish where the column time j exceeds the row time m. `multiplicity`: powers of two. For each flavour f, s -> connection[s, f] is an involution without fixed points; two states that flavour f links differ in that flavour's occupation, under a numbering of the states drawn from the seed.
All inputs are finite; a program needn't handle non-finite values.
Results may differ from the reference program's by a relative error of at most 0.012.
Values may be sent and summed in bfloat16 or wider, within the bound.
A program may use at most 64 MiB of HBM per device.

```python
import math
import jax
import jax.numpy as jnp
from jax import lax

ORB = 3
FLAV = 6
STATES = 64
K_DEV = 128
TIMES = 32
KPTS = 512
N_KA = 4


def draw_kernel_row(key, part):
    first, second = jax.random.split(jax.random.fold_in(key, 11), 2)
    spread = 0.6 / math.sqrt(3.0 * TIMES)
    common = jax.random.normal(first, (TIMES, 2, 3, 3, 1), jnp.float32)
    own = jax.random.normal(second, (TIMES, 2, 3, 3, KPTS), jnp.float32)
    values = (common + own) * spread
    return jnp.clip(values, -0.5, 0.5).astype(jnp.bfloat16)


def causal_mask(length):
    rows = jnp.arange(length, dtype=jnp.int32)
    return (rows[None, :] <= rows[:, None]).astype(jnp.float32)


def draw_lattice_history(key, part):
    first, second = jax.random.split(jax.random.fold_in(key, 23), 2)
    common = jax.random.normal(first, (TIMES, 2, 3, 3, TIMES, 1), jnp.float32)
    own = jax.random.normal(second, (TIMES, 2, 3, 3, TIMES, KPTS), jnp.float32)
    values = 0.7 * common + 0.7 * own
    mask = causal_mask(TIMES)[:, None, None, None, :, None]
    return (jnp.clip(values, -6.0, 6.0) * mask).astype(jnp.bfloat16)


def draw_pseudo_history(key, part):
    first = jax.random.fold_in(jax.random.fold_in(key, 37), 0)
    values = jax.random.normal(first, (TIMES, 2, STATES, TIMES), jnp.float32)
    mask = causal_mask(TIMES)[:, None, None, :]
    return (jnp.clip(values, -6.0, 6.0) * mask).astype(jnp.bfloat16)


def draw_diagonal_inverse(key, part):
    first, second, third = jax.random.split(jax.random.fold_in(key, 41), 3)
    identity = jnp.eye(3, dtype=jnp.float32)[:, :, None]
    diag_part = 0.2 * jax.random.normal(first, (3, 3, KPTS), jnp.float32)
    off_real = 0.3 * jax.random.normal(second, (3, 3, KPTS), jnp.float32)
    off_imag = 0.3 * jax.random.normal(third, (3, 3, KPTS), jnp.float32)
    part_real = identity * (1.0 + diag_part) + (1.0 - identity) * off_real
    return jnp.clip(jnp.stack([part_real, off_imag], axis=0), -3.0, 3.0)


def draw_multiplicity(key, part):
    index = jnp.arange(KPTS, dtype=jnp.int32)
    highest = 2 + 4 * index // KPTS
    powers = jax.random.randint(jax.random.fold_in(key, 53), (KPTS,), 0, highest + 1)
    return jnp.left_shift(jnp.ones((KPTS,), jnp.int32), powers)


def draw_connection(key, part):
    labels = jax.random.permutation(jax.random.fold_in(key, 67), STATES)
    positions = jnp.argsort(labels, stable=True).astype(jnp.int32)
    flips = jnp.left_shift(jnp.ones((FLAV,), jnp.int32), jnp.arange(FLAV, dtype=jnp.int32))
    target = jnp.bitwise_xor(positions[:, None], flips[None, :])
    return labels[target].astype(jnp.int32)


def block_levels(stream_key, dims, cuts, low, top_value):
    def one(axis_at, blocks):
        heights = jax.random.uniform(jax.random.fold_in(jax.random.fold_in(stream_key, 6), axis_at), (blocks,), jnp.float32, low / len(cuts), top_value / len(cuts))
        return jnp.repeat(jnp.exp(heights), dims[axis_at] // blocks).reshape((-1,) + (1,) * (len(dims) - axis_at - 1))

    factor_of = one(*cuts[0])
    for cut in cuts[1:]:
        factor_of = factor_of * one(*cut)
    return factor_of


def centred(key, extent, deviation, most, shards=(), held_as=jnp.bfloat16):
    array = deviation * jax.random.normal(key, extent, jnp.float32)
    if shards:
        array = array * block_levels(key, extent, shards, -0.22, 0.18)
    return jnp.clip(array, -most, most).astype(held_as)


def setup_inputs(seed: int = 0) -> dict:
    splits = jax.random.split(jax.random.key(seed), 11)
    step_index = jax.random.randint(splits[0], (1,), TIMES // 4 + 1, TIMES + 1).astype(jnp.int32)
    band_energy = jnp.clip(-1.0 + 4.0 * jax.random.uniform(splits[1], (TIMES, ORB, KPTS), jnp.float32) ** block_levels(splits[1], (TIMES, ORB, KPTS), ((0, 8), (2, 4)), -0.2, 0.2), -1.0, 3.0)
    kernel_row = draw_kernel_row(jax.random.fold_in(splits[10], 71), 0)
    lattice_history = draw_lattice_history(jax.random.fold_in(splits[10], 71), 0)
    diagonal_inverse = draw_diagonal_inverse(jax.random.fold_in(splits[10], 71), 0)
    multiplicity = draw_multiplicity(jax.random.fold_in(splits[10], 71), 0)
    state_energy = jnp.clip(jax.random.uniform(splits[6], (STATES,), jnp.float32, -3.0, 3.0), -3.0, 3.0)
    connection = draw_connection(jax.random.fold_in(splits[10], 71), 0)
    predicted_row = centred(splits[8], (2, STATES, TIMES), 1.0, 6.0, ((2, 8),), jnp.float32)
    pseudo_history = draw_pseudo_history(jax.random.fold_in(splits[10], 71), 0)
    return dict(step_index=step_index, band_energy=band_energy, kernel_row=kernel_row, lattice_history=lattice_history, diagonal_inverse=diagonal_inverse, multiplicity=multiplicity, state_energy=state_energy, connection=connection, predicted_row=predicted_row, pseudo_history=pseudo_history)


time_step = 0.05
coupling = 0.02


def complex_form(kernel):
    part_real = kernel[:, 0]
    part_imag = kernel[:, 1]
    upper = jnp.stack([part_real, -part_imag], axis=2)
    lower_half = jnp.stack([part_imag, part_real], axis=2)
    return jnp.stack([upper, lower_half], axis=1)


def contract(matrix, vector):
    return jnp.einsum('abk,jbck->jack', matrix, vector, precision=lax.Precision.HIGHEST)


def reference(step_index, band_energy, kernel_row, lattice_history, diagonal_inverse, multiplicity, state_energy, connection, predicted_row, pseudo_history):
    current = step_index[0]
    all_times = jnp.arange(TIMES, dtype=jnp.int32)
    before_now = (all_times < current).astype(jnp.float32)
    weight = jnp.where(all_times == 0, 0.5, 1.0).astype(jnp.float32) * before_now
    in_range = (all_times <= current).astype(jnp.float32)
    earlier = jnp.cumsum(band_energy, axis=0) - band_energy
    upto_now = jnp.sum(band_energy * before_now[:, None, None], axis=0)
    angles = time_step * (upto_now[None] - earlier)
    free_pair = jnp.stack([-jnp.sin(angles), -jnp.cos(angles)], axis=1) * in_range[:, None, None, None]
    identity = jnp.eye(3, dtype=jnp.float32)
    free_rows = free_pair[:, :, :, None, :] * identity[None, None, :, :, None]
    kernel = kernel_row.astype(jnp.float32) * weight[:, None, None, None, None]
    kernel_pairs = complex_form(kernel)
    pieces = []
    for k_block in range(N_KA):
        lower_k = k_block * K_DEV
        upper_k = lower_k + K_DEV
        pieces.append(jnp.einsum('msapbk,mpbcjk->jsack', kernel_pairs[..., lower_k:upper_k], lattice_history[..., lower_k:upper_k].astype(jnp.float32), precision=lax.Precision.HIGHEST))
    volterra_terms = jnp.concatenate(pieces, axis=4)
    right_side = volterra_terms + free_rows
    out_real = contract(diagonal_inverse[0], right_side[:, 0]) - contract(diagonal_inverse[1], right_side[:, 1])
    out_imag = contract(diagonal_inverse[0], right_side[:, 1]) + contract(diagonal_inverse[1], right_side[:, 0])
    fresh_rows = jnp.stack([out_real, out_imag], axis=1)
    lattice_row = fresh_rows.astype(jnp.bfloat16)
    weights_k = multiplicity.astype(jnp.float32)
    summed = jnp.einsum('jsack,k->sacj', fresh_rows, weights_k, precision=lax.Precision.HIGHEST)
    local_rows = summed / jnp.sum(weights_k)
    hybrid = jnp.repeat(jnp.diagonal(local_rows, axis1=1, axis2=2), 2, axis=2)
    hyb_real = hybrid[0].T
    hyb_imag = hybrid[1].T
    onehot = (connection[:, :, None] == jnp.arange(STATES, dtype=jnp.int32)[None, None, :]).astype(jnp.float32)
    reached = jnp.einsum('sft,ptm->psfm', onehot, predicted_row, precision=lax.Precision.HIGHEST)
    self_real = coupling * jnp.sum(hyb_real[None] * reached[0] - hyb_imag[None] * reached[1], axis=1)
    self_imag = coupling * jnp.sum(hyb_real[None] * reached[1] + hyb_imag[None] * reached[0], axis=1)
    wself_real = (self_real * weight[None, :]).T
    wself_imag = (self_imag * weight[None, :]).T
    hist_real = pseudo_history[:, 0].astype(jnp.float32)
    hist_imag = pseudo_history[:, 1].astype(jnp.float32)
    sum_real = jnp.sum(wself_real[:, :, None] * hist_real - wself_imag[:, :, None] * hist_imag, axis=0)
    sum_imag = jnp.sum(wself_real[:, :, None] * hist_imag + wself_imag[:, :, None] * hist_real, axis=0)
    elapsed = (current - all_times).astype(jnp.float32)
    spins = state_energy[:, None] * time_step * elapsed[None, :]
    pseudo_real = -jnp.sin(spins) * in_range[None, :] + sum_real
    pseudo_imag = -jnp.cos(spins) * in_range[None, :] + sum_imag
    pseudo_row = jnp.stack([pseudo_real, pseudo_imag], axis=0)
    return lattice_row, local_rows, pseudo_row
```

```python
import functools

import jax
import jax.numpy as jnp
from jax import lax
from jax.experimental import pallas as pl
from jax.experimental.pallas import tpu as pltpu
from jax.sharding import PartitionSpec as P

time_step = 0.05
coupling = 0.02
tile_rows = 16
highest = lax.Precision.HIGHEST


def dot_rows(left, right, precision=None):
    return lax.dot_general(
        left,
        right,
        (((1,), (1,)), ((), ())),
        precision=precision,
        preferred_element_type=jnp.float32,
    )


def eye(size, dtype):
    rows = lax.broadcasted_iota(jnp.int32, (size, size), 0)
    cols = lax.broadcasted_iota(jnp.int32, (size, size), 1)
    return jnp.where(rows == cols, 1.0, 0.0).astype(dtype)


def kernel(
    n_hist,
    n_ka,
    step_ref,
    band_ref,
    krow_ref,
    hist_ref,
    dinv_ref,
    mult_ref,
    energy_ref,
    conn_ref,
    pred_ref,
    pseudo_ref,
    lattice_out,
    local_out,
    pseudo_out,
    kw,
    stage,
    psend,
    precv,
    drep,
    frep,
    total,
    ksend,
    krecv,
    turned,
    qsend,
    qrecv,
    psend_sem,
    precv_sem,
    ksend_sem,
    krecv_sem,
    qsend_sem,
    qrecv_sem,
):
    block, orb, lanes = band_ref.shape
    times = hist_ref.shape[4]
    states = energy_ref.shape[1]
    pairs = 2 * orb * orb
    rows = pairs * block
    per_tile = tile_rows // block
    me = lax.axis_index("hist")
    my_ka = lax.axis_index("ka")

    barrier = pltpu.get_barrier_semaphore()

    def greet(hop, carry):
        pl.semaphore_signal(
            barrier, inc=1, device_id={"hist": lax.rem(me + hop, n_hist)},
            device_id_type=pl.DeviceIdType.MESH,
        )
        return carry

    lax.fori_loop(1, n_hist, greet, 0)
    for hop in range(1, n_ka):
        pl.semaphore_signal(
            barrier, inc=1, device_id={"ka": lax.rem(my_ka + hop, n_ka)},
            device_id_type=pl.DeviceIdType.MESH,
        )

    current = step_ref[0]
    first = me * block
    before = [jnp.where(first + m < current, 1.0, 0.0) for m in range(block)]
    weight = [
        jnp.where(first + m == 0, 0.5, 1.0) * before[m] for m in range(block)
    ]

    for m in range(block):
        kw[m] = krow_ref[m].astype(jnp.float32) * weight[m]

    suffix = [None] * block
    run = jnp.zeros((orb, lanes), jnp.float32)
    for m in reversed(range(block)):
        run = run + band_ref[m] * before[m]
        suffix[m] = run
    head = run.astype(jnp.bfloat16).astype(jnp.float32)
    rest = run - head
    tail = stage.shape[1] - rows
    for d in range(per_tile):
        stage[d, rows:, :] = jnp.zeros((tail, lanes), jnp.float32)
        stage[d, rows : rows + orb, :] = head
        stage[d, rows + orb : rows + 2 * orb, :] = rest

    pl.semaphore_wait(barrier, n_hist - 1 + n_ka - 1)

    def part_copy(source, target):
        return pltpu.make_async_remote_copy(
            src_ref=psend.at[target],
            dst_ref=precv.at[source],
            send_sem=psend_sem.at[target],
            recv_sem=precv_sem.at[source],
            device_id={"hist": target},
            device_id_type=pl.DeviceIdType.MESH,
        )

    def pseudo_copy(source, target):
        return pltpu.make_async_remote_copy(
            src_ref=qsend.at[target],
            dst_ref=qrecv.at[source],
            send_sem=qsend_sem.at[target],
            recv_sem=qrecv_sem.at[source],
            device_id={"hist": target},
            device_id_type=pl.DeviceIdType.MESH,
        )

    def one_tile(tile, carry):
        at = pl.ds(pl.multiple_of(tile * tile_rows, tile_rows), tile_rows)
        zero = jnp.zeros((tile_rows, lanes), jnp.float32)
        real = [[zero] * orb for _ in range(orb)]
        imag = [[zero] * orb for _ in range(orb)]
        for m in range(block):
            for b in range(orb):
                k_re = [kw[m, 0, a, pl.ds(b, 1), :] for a in range(orb)]
                k_im = [kw[m, 1, a, pl.ds(b, 1), :] for a in range(orb)]
                for c in range(orb):
                    h_re = hist_ref[m, 0, b, c, at, :].astype(jnp.float32)
                    h_im = hist_ref[m, 1, b, c, at, :].astype(jnp.float32)
                    for a in range(orb):
                        real[a][c] += k_re[a] * h_re - k_im[a] * h_im
                        imag[a][c] += k_re[a] * h_im + k_im[a] * h_re
        for a in range(orb):
            for c in range(orb):
                out_re, out_im = zero, zero
                for b in range(orb):
                    d_re = dinv_ref[0, a, pl.ds(b, 1), :]
                    d_im = dinv_ref[1, a, pl.ds(b, 1), :]
                    out_re += d_re * real[b][c] - d_im * imag[b][c]
                    out_im += d_re * imag[b][c] + d_im * real[b][c]
                for s, value in enumerate((out_re, out_im)):
                    row = ((s * orb + a) * orb + c) * block
                    for d in range(per_tile):
                        stage[d, row : row + block, :] = value[d * block : (d + 1) * block]
        for d in range(per_tile):
            target = tile * per_tile + d
            psend[target] = stage[d].astype(jnp.bfloat16)

            @pl.when(target < me)
            def _():
                part_copy(me, target).start()

        return carry

    lax.fori_loop(0, first // tile_rows + 1, one_tile, 0)

    for s in range(2):
        for a in range(orb):
            for c in range(orb):
                row = ((s * orb + a) * orb + c) * block
                drep[row : row + block, :] = jnp.broadcast_to(
                    dinv_ref[s, a, pl.ds(c, 1), :], (block, lanes)
                )
    total[rows:, :] = jnp.ones((lanes - rows, lanes), jnp.float32)
    mult = jnp.broadcast_to(mult_ref[...].astype(jnp.float32), (8, lanes))

    eye_j = eye(times, jnp.bfloat16)
    for m in range(block):
        h_re = dot_rows(eye_j, pseudo_ref[m, 0])
        h_im = dot_rows(eye_j, pseudo_ref[m, 1])
        turned[m, 0] = jnp.concatenate([h_re, h_im], axis=1)
        turned[m, 1] = jnp.concatenate([-h_im, h_re], axis=1)

    row_of = lax.broadcasted_iota(jnp.int32, (block, 2 * states), 0)
    lane_of = lax.broadcasted_iota(jnp.int32, (block, 2 * states), 1)
    row_time = first + row_of
    row_weight = jnp.where(row_time == 0, 0.5, 1.0) * jnp.where(row_time < current, 1.0, 0.0)
    conn = jnp.concatenate([conn_ref[...], conn_ref[...]], axis=0)
    reach = lax.broadcasted_iota(jnp.int32, (2 * states, states), 1)
    eye_m = eye(block, jnp.float32)
    turned_pred = [dot_rows(eye_m, pred_ref[p], highest) for p in range(2)]
    reached = []
    for a in range(orb):
        hit = jnp.where(conn[:, 2 * a : 2 * a + 1] == reach, 1.0, 0.0) + jnp.where(
            conn[:, 2 * a + 1 : 2 * a + 2] == reach, 1.0, 0.0
        )
        reached.append(
            [dot_rows(pred, hit, highest) * row_weight * coupling for pred in turned_pred]
        )
    energies = jnp.concatenate([energy_ref[...], energy_ref[...]], axis=1)
    spins = energies * time_step * (current - row_time).astype(jnp.float32)
    free_pseudo = jnp.where(lane_of < states, -jnp.sin(spins), -jnp.cos(spins))
    free_pseudo = free_pseudo * jnp.where(row_time <= current, 1.0, 0.0)

    def take_part(source, carry):
        summed, later = carry
        part_copy(source, me).wait_recv()
        got = precv[source].astype(jnp.float32)
        summed = summed + got[:rows]
        later = later + got[rows:]
        return summed, later

    own = psend[me].astype(jnp.float32)[:rows]
    summed, later = lax.fori_loop(
        me + 1, n_hist, take_part, (own, jnp.zeros((tail, lanes), jnp.float32))
    )
    later = later[:orb] + later[orb : 2 * orb]

    for c in range(orb):
        for j in range(block):
            frep[c * block + j : c * block + j + 1, :] = (
                later[c : c + 1] + suffix[j][c : c + 1]
            )
    size = orb * block
    angle = time_step * frep[:size, :]
    when = first + lax.rem(lax.broadcasted_iota(jnp.int32, (size, lanes), 0), block)
    inside = jnp.where(when <= current, 1.0, 0.0)
    free_re = -jnp.sin(angle) * inside
    free_im = -jnp.cos(angle) * inside
    for a in range(orb):
        frep[a * size : (a + 1) * size, :] = free_re
        frep[(orb + a) * size : (orb + a + 1) * size, :] = free_im
    half = rows // 2
    f_re, f_im = frep[:half, :], frep[half:, :]
    d_re, d_im = drep[:half, :], drep[half:, :]
    total[:half, :] = summed[:half] + d_re * f_re - d_im * f_im
    total[half:rows, :] = summed[half:] + d_re * f_im + d_im * f_re

    ksend[...] = dot_rows(mult, total[...], highest)

    def local_copy(source, target):
        return pltpu.make_async_remote_copy(
            src_ref=ksend,
            dst_ref=krecv.at[source],
            send_sem=ksend_sem.at[target],
            recv_sem=krecv_sem.at[source],
            device_id={"ka": target},
            device_id_type=pl.DeviceIdType.MESH,
        )

    for hop in range(1, n_ka):
        local_copy(my_ka, lax.rem(my_ka + hop, n_ka)).start()
    lattice_out[...] = total[:rows, :].astype(jnp.bfloat16)
    local = ksend[...]
    for hop in range(1, n_ka):
        source = lax.rem(my_ka + hop, n_ka)
        local_copy(source, my_ka).wait_recv()
        local = local + krecv[source]
    local = local / local[:, rows : rows + 1]
    local_out[...] = local

    lane8 = lax.broadcasted_iota(jnp.int32, local.shape, 1)
    row8 = lax.broadcasted_iota(jnp.int32, local.shape, 0)

    def diagonal(s, a):
        lane = ((s * orb + a) * orb + a) * block + row8
        picked = jnp.where((lane8 == lane) & (row8 < block), local, 0.0)
        return jnp.sum(picked, axis=1, keepdims=True)[:block]

    self_re = jnp.zeros((block, 2 * states), jnp.float32)
    self_im = self_re
    for a in range(orb):
        h_re, h_im = diagonal(0, a), diagonal(1, a)
        r_re, r_im = reached[a]
        self_re += h_re * r_re - h_im * r_im
        self_im += h_re * r_im + h_im * r_re
    part = jnp.zeros((times, 2 * states), jnp.float32)
    for m in range(block):
        part += self_re[m : m + 1] * turned[m, 0] + self_im[m : m + 1] * turned[m, 1]
    for q in range(n_hist):
        qsend[q] = part[q * block : (q + 1) * block]

    def give_pseudo(target, carry):
        pseudo_copy(me, target).start()
        return carry

    lax.fori_loop(0, me, give_pseudo, 0)

    def take_pseudo(source, value):
        pseudo_copy(source, me).wait_recv()
        return value + qrecv[source]

    pseudo_out[...] = lax.fori_loop(me + 1, n_hist, take_pseudo, free_pseudo + qsend[me])

    def settle(target, carry):
        part_copy(me, target).wait_send()
        pseudo_copy(me, target).wait_send()
        return carry

    lax.fori_loop(0, me, settle, 0)
    for hop in range(1, n_ka):
        local_copy(my_ka, lax.rem(my_ka + hop, n_ka)).wait_send()


def per_device(
    n_hist,
    n_ka,
    step_index,
    band_energy,
    kernel_row,
    lattice_history,
    diagonal_inverse,
    multiplicity,
    state_energy,
    connection,
    predicted_row,
    pseudo_history,
):
    block, orb, lanes = band_energy.shape
    times = lattice_history.shape[4]
    states = state_energy.shape[0]
    pairs = 2 * orb * orb
    rows = pairs * block
    sent_rows = -(-(rows + 2 * orb) // tile_rows) * tile_rows
    per_tile = tile_rows // block
    vmem = pl.BlockSpec(memory_space=pltpu.VMEM)
    f32, bf16 = jnp.float32, jnp.bfloat16
    dma = pltpu.SemaphoreType.DMA
    lattice, local, pseudo = pl.pallas_call(
        functools.partial(kernel, n_hist, n_ka),
        out_shape=(
            jax.ShapeDtypeStruct((rows, lanes), bf16),
            jax.ShapeDtypeStruct((8, lanes), f32),
            jax.ShapeDtypeStruct((block, 2 * states), f32),
        ),
        in_specs=[pl.BlockSpec(memory_space=pltpu.SMEM)] + [vmem] * 9,
        out_specs=(vmem, vmem, vmem),
        scratch_shapes=[
            pltpu.VMEM(kernel_row.shape, f32),
            pltpu.VMEM((per_tile, sent_rows, lanes), f32),
            pltpu.VMEM((n_hist, sent_rows, lanes), bf16),
            pltpu.VMEM((n_hist, sent_rows, lanes), bf16),
            pltpu.VMEM((rows, lanes), f32),
            pltpu.VMEM((rows, lanes), f32),
            pltpu.VMEM((lanes, lanes), f32),
            pltpu.VMEM((8, lanes), f32),
            pltpu.VMEM((n_ka, 8, lanes), f32),
            pltpu.VMEM((block, 2, times, 2 * states), f32),
            pltpu.VMEM((n_hist, block, 2 * states), f32),
            pltpu.VMEM((n_hist, block, 2 * states), f32),
            dma((n_hist,)),
            dma((n_hist,)),
            dma((n_ka,)),
            dma((n_ka,)),
            dma((n_hist,)),
            dma((n_hist,)),
        ],
        compiler_params=pltpu.CompilerParams(collective_id=0, has_side_effects=True),
    )(
        step_index,
        band_energy,
        kernel_row,
        lattice_history,
        diagonal_inverse,
        multiplicity[None],
        state_energy[None],
        connection,
        predicted_row,
        pseudo_history,
    )
    lattice_row = jnp.transpose(lattice.reshape(pairs, block, lanes), (1, 0, 2)).reshape(
        block, 2, orb, orb, lanes
    )
    local_row = local[0, :rows].reshape(2, orb, orb, block)
    pseudo_row = jnp.transpose(pseudo.reshape(block, 2, states), (1, 2, 0))
    return lattice_row, local_row, pseudo_row


def solution(mesh):
    in_specs = (
        P(),
        P("hist", None, "ka"),
        P("hist", None, None, None, "ka"),
        P("hist", None, None, None, None, "ka"),
        P(None, None, None, "ka"),
        P("ka"),
        P(),
        P(),
        P(None, None, "hist"),
        P("hist", None, None, None),
    )
    out_specs = (
        P("hist", None, None, None, "ka"),
        P(None, None, None, "hist"),
        P(None, None, "hist"),
    )
    return jax.shard_map(
        functools.partial(per_device, mesh.shape["hist"], mesh.shape["ka"]),
        mesh=mesh,
        in_specs=in_specs,
        out_specs=out_specs,
        check_vma=False,
    )
```

```python
import functools

import jax
import jax.numpy as jnp
from jax import lax
from jax.experimental import pallas as pl
from jax.experimental.pallas import tpu as pltpu
from jax.sharding import PartitionSpec as P

time_step = 0.05
coupling = 0.02
tile_rows = 16
highest = lax.Precision.HIGHEST


def dot_rows(left, right, precision=None):
    return lax.dot_general(
        left,
        right,
        (((1,), (1,)), ((), ())),
        precision=precision,
        preferred_element_type=jnp.float32,
    )


def kernel(
    n_hist,
    n_ka,
    step_ref,
    band_ref,
    krow_ref,
    hist_ref,
    dinv_ref,
    mult_ref,
    energy_ref,
    conn_ref,
    pred_ref,
    pseudo_ref,
    lattice_out,
    local_out,
    pseudo_out,
    kw,
    suffix,
    stage,
    psend,
    precv,
    drep,
    frep,
    total,
    ksend,
    krecv,
    turned,
    qsend,
    qrecv,
    psend_sem,
    precv_sem,
    ksend_sem,
    krecv_sem,
    qsend_sem,
    qrecv_sem,
):
    orb, block, lanes = band_ref.shape
    times = hist_ref.shape[4]
    states = energy_ref.shape[1]
    pairs = 2 * orb * orb
    rows = pairs * block
    per_tile = tile_rows // block
    me = lax.axis_index("hist")
    my_ka = lax.axis_index("ka")

    barrier = pltpu.get_barrier_semaphore()

    def greet(hop, carry):
        pl.semaphore_signal(
            barrier, inc=1, device_id={"hist": lax.rem(me + hop, n_hist)},
            device_id_type=pl.DeviceIdType.MESH,
        )
        return carry

    lax.fori_loop(1, n_hist, greet, 0)
    for hop in range(1, n_ka):
        pl.semaphore_signal(
            barrier, inc=1, device_id={"ka": lax.rem(my_ka + hop, n_ka)},
            device_id_type=pl.DeviceIdType.MESH,
        )

    current = step_ref[0]
    first = me * block
    before = [jnp.where(first + m < current, 1.0, 0.0) for m in range(block)]
    weight = [
        jnp.where(first + m == 0, 0.5, 1.0) * before[m] for m in range(block)
    ]

    for m in range(block):
        kw[m] = krow_ref[m].astype(jnp.float32) * weight[m]

    tail = stage.shape[1] - rows
    for d in range(per_tile):
        stage[d, rows:, :] = jnp.zeros((tail, lanes), jnp.float32)
    for c in range(orb):
        run = jnp.zeros((1, lanes), jnp.float32)
        for m in reversed(range(block)):
            run = run + band_ref[c, m : m + 1, :] * before[m]
            suffix[c * block + m : c * block + m + 1, :] = run
        head = run.astype(jnp.bfloat16).astype(jnp.float32)
        rest = run - head
        for d in range(per_tile):
            stage[d, rows + c : rows + c + 1, :] = head
            stage[d, rows + orb + c : rows + orb + c + 1, :] = rest

    pl.semaphore_wait(barrier, n_hist - 1 + n_ka - 1)

    def part_copy(source, target):
        return pltpu.make_async_remote_copy(
            src_ref=psend.at[target],
            dst_ref=precv.at[source],
            send_sem=psend_sem.at[target],
            recv_sem=precv_sem.at[source],
            device_id={"hist": target},
            device_id_type=pl.DeviceIdType.MESH,
        )

    def pseudo_copy(source, target):
        return pltpu.make_async_remote_copy(
            src_ref=qsend.at[target],
            dst_ref=qrecv.at[source],
            send_sem=qsend_sem.at[target],
            recv_sem=qrecv_sem.at[source],
            device_id={"hist": target},
            device_id_type=pl.DeviceIdType.MESH,
        )

    def one_tile(tile, carry):
        at = pl.ds(pl.multiple_of(tile * tile_rows, tile_rows), tile_rows)
        zero = jnp.zeros((tile_rows, lanes), jnp.float32)
        real = [[zero] * orb for _ in range(orb)]
        imag = [[zero] * orb for _ in range(orb)]
        for m in range(block):
            for b in range(orb):
                k_re = [kw[m, a, b, 0:1, :] for a in range(orb)]
                k_im = [kw[m, a, b, 1:2, :] for a in range(orb)]
                for c in range(orb):
                    h_re = hist_ref[m, 0, b, c, at, :].astype(jnp.float32)
                    h_im = hist_ref[m, 1, b, c, at, :].astype(jnp.float32)
                    for a in range(orb):
                        real[a][c] += k_re[a] * h_re - k_im[a] * h_im
                        imag[a][c] += k_re[a] * h_im + k_im[a] * h_re
        for a in range(orb):
            for c in range(orb):
                out_re, out_im = zero, zero
                for b in range(orb):
                    d_re = dinv_ref[a, b, 0:1, :]
                    d_im = dinv_ref[a, b, 1:2, :]
                    out_re += d_re * real[b][c] - d_im * imag[b][c]
                    out_im += d_re * imag[b][c] + d_im * real[b][c]
                for s, value in enumerate((out_re, out_im)):
                    row = ((s * orb + a) * orb + c) * block
                    for d in range(per_tile):
                        stage[d, row : row + block, :] = value[d * block : (d + 1) * block]
        for d in range(per_tile):
            target = tile * per_tile + d
            psend[target] = stage[d].astype(jnp.bfloat16)

            @pl.when(target < me)
            def _():
                part_copy(me, target).start()

        return carry

    lax.fori_loop(0, first // tile_rows + 1, one_tile, 0)

    for s in range(2):
        for a in range(orb):
            for c in range(orb):
                row = ((s * orb + a) * orb + c) * block
                drep[row : row + block, :] = jnp.broadcast_to(
                    dinv_ref[a, c, s : s + 1, :], (block, lanes)
                )
    total[rows:, :] = jnp.ones((lanes - rows, lanes), jnp.float32)
    mult = jnp.broadcast_to(mult_ref[...].astype(jnp.float32), (8, lanes))

    for m in range(block):
        h_re = pseudo_ref[m, 0].astype(jnp.float32)
        h_im = pseudo_ref[m, 1].astype(jnp.float32)
        turned[m, 0] = jnp.concatenate([h_re, h_im], axis=1)
        turned[m, 1] = jnp.concatenate([-h_im, h_re], axis=1)

    row_of = lax.broadcasted_iota(jnp.int32, (block, 2 * states), 0)
    lane_of = lax.broadcasted_iota(jnp.int32, (block, 2 * states), 1)
    row_time = first + row_of
    row_weight = jnp.where(row_time == 0, 0.5, 1.0) * jnp.where(row_time < current, 1.0, 0.0)
    conn = jnp.concatenate([conn_ref[...], conn_ref[...]], axis=1)
    reach = lax.broadcasted_iota(jnp.int32, (states, 2 * states), 0)
    reached = []
    for a in range(orb):
        hit = jnp.where(conn[2 * a : 2 * a + 1] == reach, 1.0, 0.0) + jnp.where(
            conn[2 * a + 1 : 2 * a + 2] == reach, 1.0, 0.0
        )
        reached.append(
            [
                jnp.dot(pred_ref[p], hit, precision=highest, preferred_element_type=jnp.float32)
                * row_weight
                * coupling
                for p in range(2)
            ]
        )
    energies = jnp.concatenate([energy_ref[...], energy_ref[...]], axis=1)
    spins = energies * time_step * (current - row_time).astype(jnp.float32)
    free_pseudo = jnp.where(lane_of < states, -jnp.sin(spins), -jnp.cos(spins))
    free_pseudo = free_pseudo * jnp.where(row_time <= current, 1.0, 0.0)

    def take_part(source, carry):
        summed, later = carry
        part_copy(source, me).wait_recv()
        got = precv[source].astype(jnp.float32)
        summed = summed + got[:rows]
        later = later + got[rows:]
        return summed, later

    own = psend[me].astype(jnp.float32)[:rows]
    summed, later = lax.fori_loop(
        me + 1, n_hist, take_part, (own, jnp.zeros((tail, lanes), jnp.float32))
    )
    later = later[:orb] + later[orb : 2 * orb]

    for c in range(orb):
        for j in range(block):
            frep[c * block + j : c * block + j + 1, :] = (
                later[c : c + 1] + suffix[c * block + j : c * block + j + 1, :]
            )
    size = orb * block
    angle = time_step * frep[:size, :]
    when = first + lax.rem(lax.broadcasted_iota(jnp.int32, (size, lanes), 0), block)
    inside = jnp.where(when <= current, 1.0, 0.0)
    free_re = -jnp.sin(angle) * inside
    free_im = -jnp.cos(angle) * inside
    for a in range(orb):
        frep[a * size : (a + 1) * size, :] = free_re
        frep[(orb + a) * size : (orb + a + 1) * size, :] = free_im
    half = rows // 2
    f_re, f_im = frep[:half, :], frep[half:, :]
    d_re, d_im = drep[:half, :], drep[half:, :]
    total[:half, :] = summed[:half] + d_re * f_re - d_im * f_im
    total[half:rows, :] = summed[half:] + d_re * f_im + d_im * f_re

    ksend[...] = dot_rows(mult, total[...], highest)

    def local_copy(source, target):
        return pltpu.make_async_remote_copy(
            src_ref=ksend,
            dst_ref=krecv.at[source],
            send_sem=ksend_sem.at[target],
            recv_sem=krecv_sem.at[source],
            device_id={"ka": target},
            device_id_type=pl.DeviceIdType.MESH,
        )

    for hop in range(1, n_ka):
        local_copy(my_ka, lax.rem(my_ka + hop, n_ka)).start()
    for a in range(orb):
        for c in range(orb):
            for j in range(block):
                pair = total[pl.ds((a * orb + c) * block + j, 2, stride=half), :]
                lattice_out[j, a, c] = pair.astype(jnp.bfloat16)
    local = ksend[...]
    for hop in range(1, n_ka):
        source = lax.rem(my_ka + hop, n_ka)
        local_copy(source, my_ka).wait_recv()
        local = local + krecv[source]
    local = local / local[:, rows : rows + 1]

    lane8 = lax.broadcasted_iota(jnp.int32, local.shape, 1)
    row8 = lax.broadcasted_iota(jnp.int32, local.shape, 0)

    def diagonal(s, a):
        lane = ((s * orb + a) * orb + a) * block + row8
        picked = jnp.where((lane8 == lane) & (row8 < block), local, 0.0)
        return jnp.sum(picked, axis=1, keepdims=True)[:block]

    self_re = jnp.zeros((block, 2 * states), jnp.float32)
    self_im = self_re
    for a in range(orb):
        h_re, h_im = diagonal(0, a), diagonal(1, a)
        r_re, r_im = reached[a]
        self_re += h_re * r_re - h_im * r_im
        self_im += h_re * r_im + h_im * r_re
    part = jnp.zeros((times, 2 * states), jnp.float32)
    for m in range(block):
        part += self_re[m : m + 1] * turned[m, 0] + self_im[m : m + 1] * turned[m, 1]
    for q in range(n_hist):
        qsend[q] = part[q * block : (q + 1) * block]

    def give_pseudo(target, carry):
        pseudo_copy(me, target).start()
        return carry

    lax.fori_loop(0, me, give_pseudo, 0)

    for s in range(2):
        for a in range(orb):
            for c in range(orb):
                row = ((s * orb + a) * orb + c) * block
                local_out[a, c, s : s + 1, :] = local[0:1, row : row + block]

    def take_pseudo(source, value):
        pseudo_copy(source, me).wait_recv()
        return value + qrecv[source]

    value = lax.fori_loop(me + 1, n_hist, take_pseudo, free_pseudo + qsend[me])
    for p in range(2):
        pseudo_out[p] = value[:, p * states : (p + 1) * states]

    def settle(target, carry):
        part_copy(me, target).wait_send()
        pseudo_copy(me, target).wait_send()
        return carry

    lax.fori_loop(0, me, settle, 0)
    for hop in range(1, n_ka):
        local_copy(my_ka, lax.rem(my_ka + hop, n_ka)).wait_send()


def per_device(
    n_hist,
    n_ka,
    step_index,
    band_energy,
    kernel_row,
    lattice_history,
    diagonal_inverse,
    multiplicity,
    state_energy,
    connection,
    predicted_row,
    pseudo_history,
):
    block, orb, lanes = band_energy.shape
    times = lattice_history.shape[4]
    states = state_energy.shape[0]
    pairs = 2 * orb * orb
    rows = pairs * block
    sent_rows = -(-(rows + 2 * orb) // tile_rows) * tile_rows
    per_tile = tile_rows // block
    vmem = pl.BlockSpec(memory_space=pltpu.VMEM)
    f32, bf16 = jnp.float32, jnp.bfloat16
    dma = pltpu.SemaphoreType.DMA
    lattice, local, pseudo = pl.pallas_call(
        functools.partial(kernel, n_hist, n_ka),
        out_shape=(
            jax.ShapeDtypeStruct((block, orb, orb, 2, lanes), bf16),
            jax.ShapeDtypeStruct((orb, orb, 2, block), f32),
            jax.ShapeDtypeStruct((2, block, states), f32),
        ),
        in_specs=[pl.BlockSpec(memory_space=pltpu.SMEM)] + [vmem] * 9,
        out_specs=(vmem, vmem, vmem),
        scratch_shapes=[
            pltpu.VMEM((block, orb, orb, 2, lanes), f32),
            pltpu.VMEM((orb * block, lanes), f32),
            pltpu.VMEM((per_tile, sent_rows, lanes), f32),
            pltpu.VMEM((n_hist, sent_rows, lanes), bf16),
            pltpu.VMEM((n_hist, sent_rows, lanes), bf16),
            pltpu.VMEM((rows, lanes), f32),
            pltpu.VMEM((rows, lanes), f32),
            pltpu.VMEM((lanes, lanes), f32),
            pltpu.VMEM((8, lanes), f32),
            pltpu.VMEM((n_ka, 8, lanes), f32),
            pltpu.VMEM((block, 2, times, 2 * states), f32),
            pltpu.VMEM((n_hist, block, 2 * states), f32),
            pltpu.VMEM((n_hist, block, 2 * states), f32),
            dma((n_hist,)),
            dma((n_hist,)),
            dma((n_ka,)),
            dma((n_ka,)),
            dma((n_hist,)),
            dma((n_hist,)),
        ],
        compiler_params=pltpu.CompilerParams(collective_id=0, has_side_effects=True),
    )(
        step_index,
        jnp.transpose(band_energy, (1, 0, 2)),
        jnp.transpose(kernel_row, (0, 2, 3, 1, 4)),
        lattice_history,
        jnp.transpose(diagonal_inverse, (1, 2, 0, 3)),
        multiplicity[None],
        state_energy[None],
        jnp.transpose(connection),
        jnp.transpose(predicted_row, (0, 2, 1)),
        jnp.transpose(pseudo_history, (0, 1, 3, 2)),
    )
    return (
        jnp.transpose(lattice, (0, 3, 1, 2, 4)),
        jnp.transpose(local, (2, 0, 1, 3)),
        jnp.transpose(pseudo, (0, 2, 1)),
    )


def solution(mesh):
    in_specs = (
        P(),
        P("hist", None, "ka"),
        P("hist", None, None, None, "ka"),
        P("hist", None, None, None, None, "ka"),
        P(None, None, None, "ka"),
        P("ka"),
        P(),
        P(),
        P(None, None, "hist"),
        P("hist", None, None, None),
    )
    out_specs = (
        P("hist", None, None, None, "ka"),
        P(None, None, None, "hist"),
        P(None, None, "hist"),
    )
    return jax.shard_map(
        functools.partial(per_device, mesh.shape["hist"], mesh.shape["ka"]),
        mesh=mesh,
        in_specs=in_specs,
        out_specs=out_specs,
        check_vma=False,
    )
```

```python
import functools

import jax
import jax.numpy as jnp
from jax import lax
from jax.experimental import pallas as pl
from jax.experimental.pallas import tpu as pltpu
from jax.sharding import PartitionSpec as P

time_step = 0.05
coupling = 0.02
tile_rows = 16
highest = lax.Precision.HIGHEST


def dot_rows(left, right, precision=None):
    return lax.dot_general(
        left,
        right,
        (((1,), (1,)), ((), ())),
        precision=precision,
        preferred_element_type=jnp.float32,
    )


def kernel(
    n_hist,
    n_ka,
    step_ref,
    band_ref,
    krow_ref,
    hist_ref,
    dinv_ref,
    mult_ref,
    energy_ref,
    conn_ref,
    pred_ref,
    pseudo_ref,
    total_out,
    local_out,
    pseudo_out,
    hist_vmem,
    kw,
    suffix,
    stage,
    esend,
    erecv,
    lsend,
    lrecv,
    psend,
    precv,
    drep,
    frep,
    total,
    ksend,
    krecv,
    turned,
    qsend,
    qrecv,
    hist_sem,
    esend_sem,
    erecv_sem,
    lsend_sem,
    lrecv_sem,
    psend_sem,
    precv_sem,
    ksend_sem,
    krecv_sem,
    qsend_sem,
    qrecv_sem,
):
    orb, block, lanes = band_ref.shape
    times = hist_ref.shape[4]
    states = energy_ref.shape[1]
    pairs = 2 * orb * orb
    rows = pairs * block
    per_tile = tile_rows // block
    me = lax.axis_index("hist")
    my_ka = lax.axis_index("ka")

    load = pltpu.make_async_copy(hist_ref, hist_vmem, hist_sem)
    load.start()
    barrier = pltpu.get_barrier_semaphore()

    def greet(hop, carry):
        pl.semaphore_signal(
            barrier, inc=1, device_id={"hist": lax.rem(me + hop, n_hist)},
            device_id_type=pl.DeviceIdType.MESH,
        )
        return carry

    lax.fori_loop(1, n_hist, greet, 0)
    for hop in range(1, n_ka):
        pl.semaphore_signal(
            barrier, inc=1, device_id={"ka": lax.rem(my_ka + hop, n_ka)},
            device_id_type=pl.DeviceIdType.MESH,
        )

    current = step_ref[0]
    first = me * block
    before = [jnp.where(first + m < current, 1.0, 0.0) for m in range(block)]
    weight = [
        jnp.where(first + m == 0, 0.5, 1.0) * before[m] for m in range(block)
    ]

    for m in range(block):
        kw[m] = krow_ref[m].astype(jnp.float32) * weight[m]

    esend[...] = jnp.zeros(esend.shape, jnp.float32)
    for c in range(orb):
        run = jnp.zeros((1, lanes), jnp.float32)
        for m in reversed(range(block)):
            run = run + band_ref[c, m : m + 1, :] * before[m]
            suffix[c * block + m : c * block + m + 1, :] = run
        esend[c : c + 1, :] = run
    mult = jnp.broadcast_to(mult_ref[...].astype(jnp.float32), (8, lanes))

    pl.semaphore_wait(barrier, n_hist - 1 + n_ka - 1)

    def hist_copy(src, dst, send_sem, recv_sem, source, target):
        return pltpu.make_async_remote_copy(
            src_ref=src,
            dst_ref=dst.at[source],
            send_sem=send_sem.at[target],
            recv_sem=recv_sem.at[source],
            device_id={"hist": target},
            device_id_type=pl.DeviceIdType.MESH,
        )

    def energy_copy(source, target):
        return hist_copy(esend, erecv, esend_sem, erecv_sem, source, target)

    def sum_copy(source, target):
        return hist_copy(lsend.at[target], lrecv, lsend_sem, lrecv_sem, source, target)

    def part_copy(source, target):
        return hist_copy(psend.at[target], precv, psend_sem, precv_sem, source, target)

    def pseudo_copy(source, target):
        return hist_copy(qsend.at[target], qrecv, qsend_sem, qrecv_sem, source, target)

    def give_energy(target, carry):
        energy_copy(me, target).start()
        return carry

    lax.fori_loop(0, me, give_energy, 0)
    load.wait()

    def one_tile(tile, carry):
        at = pl.ds(pl.multiple_of(tile * tile_rows, tile_rows), tile_rows)
        zero = jnp.zeros((tile_rows, lanes), jnp.float32)
        real = [[zero] * orb for _ in range(orb)]
        imag = [[zero] * orb for _ in range(orb)]
        for m in range(block):
            for b in range(orb):
                k_re = [kw[m, a, b, 0:1, :] for a in range(orb)]
                k_im = [kw[m, a, b, 1:2, :] for a in range(orb)]
                for c in range(orb):
                    h_re = hist_vmem[m, 0, b, c, at, :].astype(jnp.float32)
                    h_im = hist_vmem[m, 1, b, c, at, :].astype(jnp.float32)
                    for a in range(orb):
                        real[a][c] += k_re[a] * h_re - k_im[a] * h_im
                        imag[a][c] += k_re[a] * h_im + k_im[a] * h_re
        for a in range(orb):
            for c in range(orb):
                out_re, out_im = zero, zero
                for b in range(orb):
                    d_re = dinv_ref[a, b, 0:1, :]
                    d_im = dinv_ref[a, b, 1:2, :]
                    out_re += d_re * real[b][c] - d_im * imag[b][c]
                    out_im += d_re * imag[b][c] + d_im * real[b][c]
                for s, value in enumerate((out_re, out_im)):
                    row = ((s * orb + a) * orb + c) * block
                    for d in range(per_tile):
                        stage[d, row : row + block, :] = value[d * block : (d + 1) * block]
        for d in range(per_tile):
            target = tile * per_tile + d
            lsend[target, :, :rows] = dot_rows(mult, stage[d], highest)[:1]

            @pl.when(target < me)
            def _():
                sum_copy(me, target).start()

        for d in range(per_tile):
            psend[tile * per_tile + d] = stage[d].astype(jnp.bfloat16)
        return carry

    lax.fori_loop(0, first // tile_rows + 1, one_tile, 0)

    def give_part(target, carry):
        part_copy(me, target).start()
        return carry

    lax.fori_loop(0, me, give_part, 0)

    for s in range(2):
        for a in range(orb):
            for c in range(orb):
                row = ((s * orb + a) * orb + c) * block
                drep[row : row + block, :] = jnp.broadcast_to(
                    dinv_ref[a, c, s : s + 1, :], (block, lanes)
                )
    total[rows:, :] = jnp.ones((lanes - rows, lanes), jnp.float32)
    for m in range(block):
        h_re = pseudo_ref[m, 0].astype(jnp.float32)
        h_im = pseudo_ref[m, 1].astype(jnp.float32)
        turned[m, 0] = jnp.concatenate([h_re, h_im], axis=1)
        turned[m, 1] = jnp.concatenate([-h_im, h_re], axis=1)

    row_of = lax.broadcasted_iota(jnp.int32, (block, 2 * states), 0)
    lane_of = lax.broadcasted_iota(jnp.int32, (block, 2 * states), 1)
    row_time = first + row_of
    row_weight = jnp.where(row_time == 0, 0.5, 1.0) * jnp.where(row_time < current, 1.0, 0.0)
    conn = jnp.concatenate([conn_ref[...], conn_ref[...]], axis=1)
    reach = lax.broadcasted_iota(jnp.int32, (states, 2 * states), 0)
    reached = []
    for a in range(orb):
        hit = jnp.where(conn[2 * a : 2 * a + 1] == reach, 1.0, 0.0) + jnp.where(
            conn[2 * a + 1 : 2 * a + 2] == reach, 1.0, 0.0
        )
        reached.append(
            [
                jnp.dot(pred_ref[p], hit, precision=highest, preferred_element_type=jnp.float32)
                * row_weight
                * coupling
                for p in range(2)
            ]
        )
    energies = jnp.concatenate([energy_ref[...], energy_ref[...]], axis=1)
    spins = energies * time_step * (current - row_time).astype(jnp.float32)
    free_pseudo = jnp.where(lane_of < states, -jnp.sin(spins), -jnp.cos(spins))
    free_pseudo = free_pseudo * jnp.where(row_time <= current, 1.0, 0.0)

    def take_energy(source, later):
        energy_copy(source, me).wait_recv()
        return later + erecv[source]

    later = lax.fori_loop(
        me + 1, n_hist, take_energy, jnp.zeros(esend.shape, jnp.float32)
    )
    for c in range(orb):
        for j in range(block):
            frep[c * block + j : c * block + j + 1, :] = (
                later[c : c + 1] + suffix[c * block + j : c * block + j + 1, :]
            )
    size = orb * block
    angle = time_step * frep[:size, :]
    when = first + lax.rem(lax.broadcasted_iota(jnp.int32, (size, lanes), 0), block)
    inside = jnp.where(when <= current, 1.0, 0.0)
    free_re = -jnp.sin(angle) * inside
    free_im = -jnp.cos(angle) * inside
    for a in range(orb):
        frep[a * size : (a + 1) * size, :] = free_re
        frep[(orb + a) * size : (orb + a + 1) * size, :] = free_im
    half = rows // 2
    f_re, f_im = frep[:half, :], frep[half:, :]
    d_re, d_im = drep[:half, :], drep[half:, :]
    total[:half, :] = d_re * f_re - d_im * f_im
    total[half:rows, :] = d_re * f_im + d_im * f_re

    free_sums = dot_rows(mult, total[...], highest)[:1]

    def take_sum(source, value):
        sum_copy(source, me).wait_recv()
        return value + lrecv[source][:, :rows]

    own_sums = lsend[me][:, :rows] + free_sums[:, :rows]
    ksend[...] = free_sums
    ksend[:, :rows] = lax.fori_loop(me + 1, n_hist, take_sum, own_sums)

    def local_copy(source, target):
        return pltpu.make_async_remote_copy(
            src_ref=ksend,
            dst_ref=krecv.at[source],
            send_sem=ksend_sem.at[target],
            recv_sem=krecv_sem.at[source],
            device_id={"ka": target},
            device_id_type=pl.DeviceIdType.MESH,
        )

    for hop in range(1, n_ka):
        local_copy(my_ka, lax.rem(my_ka + hop, n_ka)).start()
    local = ksend[...]
    for hop in range(1, n_ka):
        source = lax.rem(my_ka + hop, n_ka)
        local_copy(source, my_ka).wait_recv()
        local = local + krecv[source]
    local = jnp.broadcast_to(local / local[:, rows : rows + 1], (8, lanes))
    local_out[...] = local

    lane8 = lax.broadcasted_iota(jnp.int32, local.shape, 1)
    row8 = lax.broadcasted_iota(jnp.int32, local.shape, 0)

    def diagonal(s, a):
        lane = ((s * orb + a) * orb + a) * block + row8
        picked = jnp.where((lane8 == lane) & (row8 < block), local, 0.0)
        return jnp.sum(picked, axis=1, keepdims=True)[:block]

    self_re = jnp.zeros((block, 2 * states), jnp.float32)
    self_im = self_re
    for a in range(orb):
        h_re, h_im = diagonal(0, a), diagonal(1, a)
        r_re, r_im = reached[a]
        self_re += h_re * r_re - h_im * r_im
        self_im += h_re * r_im + h_im * r_re
    part = jnp.zeros((times, 2 * states), jnp.float32)
    for m in range(block):
        part += self_re[m : m + 1] * turned[m, 0] + self_im[m : m + 1] * turned[m, 1]
    for q in range(n_hist):
        qsend[q] = part[q * block : (q + 1) * block]

    def give_pseudo(target, carry):
        pseudo_copy(me, target).start()
        return carry

    lax.fori_loop(0, me, give_pseudo, 0)

    def take_part(source, value):
        part_copy(source, me).wait_recv()
        return value + precv[source].astype(jnp.float32)

    fresh = total[:rows, :] + psend[me].astype(jnp.float32)
    total_out[...] = lax.fori_loop(me + 1, n_hist, take_part, fresh)

    def take_pseudo(source, value):
        pseudo_copy(source, me).wait_recv()
        return value + qrecv[source]

    pseudo_out[...] = lax.fori_loop(me + 1, n_hist, take_pseudo, free_pseudo + qsend[me])

    def settle(target, carry):
        energy_copy(me, target).wait_send()
        sum_copy(me, target).wait_send()
        part_copy(me, target).wait_send()
        pseudo_copy(me, target).wait_send()
        return carry

    lax.fori_loop(0, me, settle, 0)
    for hop in range(1, n_ka):
        local_copy(my_ka, lax.rem(my_ka + hop, n_ka)).wait_send()


def lay_out(total_ref, local_ref, pseudo_ref, lattice_out, local_out, pseudo_out):
    block, orb = lattice_out.shape[:2]
    states = pseudo_out.shape[2]
    half = total_ref.shape[0] // 2
    for a in range(orb):
        for c in range(orb):
            row = (a * orb + c) * block
            for j in range(block):
                pair = total_ref[pl.ds(row + j, 2, stride=half), :]
                lattice_out[j, a, c] = pair.astype(jnp.bfloat16)
            for s in range(2):
                at = s * half + row
                local_out[a, c, s : s + 1, :] = local_ref[0:1, at : at + block]
    for p in range(2):
        pseudo_out[p] = pseudo_ref[:, p * states : (p + 1) * states]


def per_device(
    n_hist,
    n_ka,
    step_index,
    band_energy,
    kernel_row,
    lattice_history,
    diagonal_inverse,
    multiplicity,
    state_energy,
    connection,
    predicted_row,
    pseudo_history,
):
    block, orb, lanes = band_energy.shape
    times = lattice_history.shape[4]
    states = state_energy.shape[0]
    pairs = 2 * orb * orb
    rows = pairs * block
    per_tile = tile_rows // block
    vmem = pl.BlockSpec(memory_space=pltpu.VMEM)
    f32, bf16 = jnp.float32, jnp.bfloat16
    dma = pltpu.SemaphoreType.DMA
    results = pl.pallas_call(
        functools.partial(kernel, n_hist, n_ka),
        out_shape=(
            jax.ShapeDtypeStruct((rows, lanes), f32),
            jax.ShapeDtypeStruct((8, lanes), f32),
            jax.ShapeDtypeStruct((block, 2 * states), f32),
        ),
        in_specs=[pl.BlockSpec(memory_space=pltpu.SMEM)] + [vmem] * 2
        + [pl.BlockSpec(memory_space=pl.ANY)] + [vmem] * 6,
        out_specs=(vmem, vmem, vmem),
        scratch_shapes=[
            pltpu.VMEM(lattice_history.shape, bf16),
            pltpu.VMEM((block, orb, orb, 2, lanes), f32),
            pltpu.VMEM((orb * block, lanes), f32),
            pltpu.VMEM((per_tile, rows, lanes), f32),
            pltpu.VMEM((8, lanes), f32),
            pltpu.VMEM((n_hist, 8, lanes), f32),
            pltpu.VMEM((n_hist, 1, lanes), f32),
            pltpu.VMEM((n_hist, 1, lanes), f32),
            pltpu.VMEM((n_hist, rows, lanes), bf16),
            pltpu.VMEM((n_hist, rows, lanes), bf16),
            pltpu.VMEM((rows, lanes), f32),
            pltpu.VMEM((rows, lanes), f32),
            pltpu.VMEM((lanes, lanes), f32),
            pltpu.VMEM((1, lanes), f32),
            pltpu.VMEM((n_ka, 1, lanes), f32),
            pltpu.VMEM((block, 2, times, 2 * states), f32),
            pltpu.VMEM((n_hist, block, 2 * states), f32),
            pltpu.VMEM((n_hist, block, 2 * states), f32),
            dma,
            dma((n_hist,)),
            dma((n_hist,)),
            dma((n_hist,)),
            dma((n_hist,)),
            dma((n_hist,)),
            dma((n_hist,)),
            dma((n_ka,)),
            dma((n_ka,)),
            dma((n_hist,)),
            dma((n_hist,)),
        ],
        compiler_params=pltpu.CompilerParams(collective_id=0, has_side_effects=True),
    )(
        step_index,
        jnp.transpose(band_energy, (1, 0, 2)),
        jnp.transpose(kernel_row, (0, 2, 3, 1, 4)),
        lattice_history,
        jnp.transpose(diagonal_inverse, (1, 2, 0, 3)),
        multiplicity[None],
        state_energy[None],
        jnp.transpose(connection),
        jnp.transpose(predicted_row, (0, 2, 1)),
        jnp.transpose(pseudo_history, (0, 1, 3, 2)),
    )
    lattice, local, pseudo = pl.pallas_call(
        lay_out,
        out_shape=(
            jax.ShapeDtypeStruct((block, orb, orb, 2, lanes), bf16),
            jax.ShapeDtypeStruct((orb, orb, 2, block), f32),
            jax.ShapeDtypeStruct((2, block, states), f32),
        ),
        in_specs=[vmem] * 3,
        out_specs=(vmem, vmem, vmem),
    )(*results)
    return (
        jnp.transpose(lattice, (0, 3, 1, 2, 4)),
        jnp.transpose(local, (2, 0, 1, 3)),
        jnp.transpose(pseudo, (0, 2, 1)),
    )


def solution(mesh):
    in_specs = (
        P(),
        P("hist", None, "ka"),
        P("hist", None, None, None, "ka"),
        P("hist", None, None, None, None, "ka"),
        P(None, None, None, "ka"),
        P("ka"),
        P(),
        P(),
        P(None, None, "hist"),
        P("hist", None, None, None),
    )
    out_specs = (
        P("hist", None, None, None, "ka"),
        P(None, None, None, "hist"),
        P(None, None, "hist"),
    )
    return jax.shard_map(
        functools.partial(per_device, mesh.shape["hist"], mesh.shape["ka"]),
        mesh=mesh,
        in_specs=in_specs,
        out_specs=out_specs,
        check_vma=False,
    )
```

```python
import functools

import jax
import jax.numpy as jnp
from jax import lax
from jax.experimental import pallas as pl
from jax.experimental.pallas import tpu as pltpu
from jax.sharding import PartitionSpec as P

time_step = 0.05
coupling = 0.02
tile_rows = 16
highest = lax.Precision.HIGHEST


def weighted_sums(mult, values):
    upper = values.astype(jnp.bfloat16)
    lower = (values - upper.astype(jnp.float32)).astype(jnp.bfloat16)
    return dot_rows(mult, upper) + dot_rows(mult, lower)


def dot_rows(left, right, precision=None):
    return lax.dot_general(
        left,
        right,
        (((1,), (1,)), ((), ())),
        precision=precision,
        preferred_element_type=jnp.float32,
    )


def kernel(
    n_hist,
    n_ka,
    step_ref,
    band_any,
    krow_any,
    hist_any,
    dinv_any,
    mult_any,
    energy_any,
    conn_any,
    pred_any,
    pseudo_any,
    total_out,
    local_out,
    pseudo_out,
    band_ref,
    krow_ref,
    hist_ref,
    dinv_ref,
    mult_ref,
    energy_ref,
    conn_ref,
    pred_ref,
    pseudo_ref,
    kw,
    suffix,
    stage,
    esend,
    erecv,
    lsend,
    lrecv,
    psend,
    precv,
    drep,
    frep,
    total,
    ksend,
    krecv,
    turned,
    qsend,
    qrecv,
    load_sem,
    esend_sem,
    erecv_sem,
    lsend_sem,
    lrecv_sem,
    psend_sem,
    precv_sem,
    ksend_sem,
    krecv_sem,
    qsend_sem,
    qrecv_sem,
):
    orb, block, lanes = band_ref.shape
    times = hist_ref.shape[4]
    states = energy_ref.shape[1]
    pairs = 2 * orb * orb
    rows = pairs * block
    per_tile = tile_rows // block
    me = lax.axis_index("hist")
    my_ka = lax.axis_index("ka")

    barrier = pltpu.get_barrier_semaphore()

    def greet(hop, carry):
        pl.semaphore_signal(
            barrier, inc=1, device_id={"hist": lax.rem(me + hop, n_hist)},
            device_id_type=pl.DeviceIdType.MESH,
        )
        return carry

    lax.fori_loop(1, n_hist, greet, 0)
    for hop in range(1, n_ka):
        pl.semaphore_signal(
            barrier, inc=1, device_id={"ka": lax.rem(my_ka + hop, n_ka)},
            device_id_type=pl.DeviceIdType.MESH,
        )

    sources = (
        krow_any, band_any, mult_any, hist_any, dinv_any, energy_any, conn_any, pred_any, pseudo_any
    )
    targets = (
        krow_ref, band_ref, mult_ref, hist_ref, dinv_ref, energy_ref, conn_ref, pred_ref, pseudo_ref
    )
    loads = [
        pltpu.make_async_copy(source, target, load_sem.at[i])
        for i, (source, target) in enumerate(zip(sources, targets))
    ]
    for load in loads:
        load.start()

    current = step_ref[0]
    first = me * block
    before = [jnp.where(first + m < current, 1.0, 0.0) for m in range(block)]
    weight = [
        jnp.where(first + m == 0, 0.5, 1.0) * before[m] for m in range(block)
    ]

    for load in loads[:3]:
        load.wait()
    for m in range(block):
        kw[m] = krow_ref[m].astype(jnp.float32) * weight[m]

    esend[...] = jnp.zeros(esend.shape, jnp.float32)
    for c in range(orb):
        run = jnp.zeros((1, lanes), jnp.float32)
        for m in reversed(range(block)):
            run = run + band_ref[c, m : m + 1, :] * before[m]
            suffix[c * block + m : c * block + m + 1, :] = run
        esend[c : c + 1, :] = run
    mult = jnp.broadcast_to(mult_ref[...].astype(jnp.float32), (8, lanes)).astype(jnp.bfloat16)

    pl.semaphore_wait(barrier, n_hist - 1 + n_ka - 1)

    def hist_copy(src, dst, send_sem, recv_sem, source, target):
        return pltpu.make_async_remote_copy(
            src_ref=src,
            dst_ref=dst.at[source],
            send_sem=send_sem.at[target],
            recv_sem=recv_sem.at[source],
            device_id={"hist": target},
            device_id_type=pl.DeviceIdType.MESH,
        )

    def energy_copy(source, target):
        return hist_copy(esend, erecv, esend_sem, erecv_sem, source, target)

    def sum_copy(source, target):
        return hist_copy(lsend.at[target], lrecv, lsend_sem, lrecv_sem, source, target)

    def part_copy(source, target):
        return hist_copy(psend.at[target], precv, psend_sem, precv_sem, source, target)

    def pseudo_copy(source, target):
        return hist_copy(qsend.at[target], qrecv, qsend_sem, qrecv_sem, source, target)

    def give_energy(target, carry):
        energy_copy(me, target).start()
        return carry

    lax.fori_loop(0, me, give_energy, 0)
    for load in loads[3:]:
        load.wait()

    def one_tile(tile, carry):
        at = pl.ds(pl.multiple_of(tile * tile_rows, tile_rows), tile_rows)
        zero = jnp.zeros((tile_rows, lanes), jnp.float32)
        real = [[zero] * orb for _ in range(orb)]
        imag = [[zero] * orb for _ in range(orb)]
        for m in range(block):
            for b in range(orb):
                k_re = [kw[m, a, b, 0:1, :] for a in range(orb)]
                k_im = [kw[m, a, b, 1:2, :] for a in range(orb)]
                for c in range(orb):
                    h_re = hist_ref[m, 0, b, c, at, :].astype(jnp.float32)
                    h_im = hist_ref[m, 1, b, c, at, :].astype(jnp.float32)
                    for a in range(orb):
                        real[a][c] += k_re[a] * h_re - k_im[a] * h_im
                        imag[a][c] += k_re[a] * h_im + k_im[a] * h_re
        for a in range(orb):
            for c in range(orb):
                out_re, out_im = zero, zero
                for b in range(orb):
                    d_re = dinv_ref[a, b, 0:1, :]
                    d_im = dinv_ref[a, b, 1:2, :]
                    out_re += d_re * real[b][c] - d_im * imag[b][c]
                    out_im += d_re * imag[b][c] + d_im * real[b][c]
                for s, value in enumerate((out_re, out_im)):
                    row = ((s * orb + a) * orb + c) * block
                    for d in range(per_tile):
                        stage[d, row : row + block, :] = value[d * block : (d + 1) * block]
        sums = weighted_sums(mult, stage[...].reshape(per_tile * rows, lanes))
        for d in range(per_tile):
            target = tile * per_tile + d
            lsend[target, :, :rows] = sums[:1, d * rows : (d + 1) * rows]

            @pl.when(target < me)
            def _():
                sum_copy(me, target).start()

        for d in range(per_tile):
            psend[tile * per_tile + d] = stage[d].astype(jnp.bfloat16)
        return carry

    lax.fori_loop(0, first // tile_rows + 1, one_tile, 0)

    def give_part(target, carry):
        part_copy(me, target).start()
        return carry

    lax.fori_loop(0, me, give_part, 0)

    for s in range(2):
        for a in range(orb):
            for c in range(orb):
                row = ((s * orb + a) * orb + c) * block
                drep[row : row + block, :] = jnp.broadcast_to(
                    dinv_ref[a, c, s : s + 1, :], (block, lanes)
                )
    total[rows:, :] = jnp.ones((lanes - rows, lanes), jnp.float32)
    for m in range(block):
        h_re = pseudo_ref[m, 0].astype(jnp.float32)
        h_im = pseudo_ref[m, 1].astype(jnp.float32)
        turned[m, 0] = jnp.concatenate([h_re, h_im], axis=1)
        turned[m, 1] = jnp.concatenate([-h_im, h_re], axis=1)

    row_of = lax.broadcasted_iota(jnp.int32, (block, 2 * states), 0)
    lane_of = lax.broadcasted_iota(jnp.int32, (block, 2 * states), 1)
    row_time = first + row_of
    row_weight = jnp.where(row_time == 0, 0.5, 1.0) * jnp.where(row_time < current, 1.0, 0.0)
    conn = jnp.concatenate([conn_ref[...], conn_ref[...]], axis=1)
    reach = lax.broadcasted_iota(jnp.int32, (states, 2 * states), 0)
    reached = []
    for a in range(orb):
        hit = jnp.where(conn[2 * a : 2 * a + 1] == reach, 1.0, 0.0) + jnp.where(
            conn[2 * a + 1 : 2 * a + 2] == reach, 1.0, 0.0
        )
        reached.append(
            [
                jnp.dot(pred_ref[p], hit, precision=highest, preferred_element_type=jnp.float32)
                * row_weight
                * coupling
                for p in range(2)
            ]
        )
    energies = jnp.concatenate([energy_ref[...], energy_ref[...]], axis=1)
    spins = energies * time_step * (current - row_time).astype(jnp.float32)
    free_pseudo = jnp.where(lane_of < states, -jnp.sin(spins), -jnp.cos(spins))
    free_pseudo = free_pseudo * jnp.where(row_time <= current, 1.0, 0.0)

    def take_energy(source, later):
        energy_copy(source, me).wait_recv()
        return later + erecv[source]

    later = lax.fori_loop(
        me + 1, n_hist, take_energy, jnp.zeros(esend.shape, jnp.float32)
    )
    for c in range(orb):
        for j in range(block):
            frep[c * block + j : c * block + j + 1, :] = (
                later[c : c + 1] + suffix[c * block + j : c * block + j + 1, :]
            )
    size = orb * block
    angle = time_step * frep[:size, :]
    when = first + lax.rem(lax.broadcasted_iota(jnp.int32, (size, lanes), 0), block)
    inside = jnp.where(when <= current, 1.0, 0.0)
    free_re = -jnp.sin(angle) * inside
    free_im = -jnp.cos(angle) * inside
    for a in range(orb):
        frep[a * size : (a + 1) * size, :] = free_re
        frep[(orb + a) * size : (orb + a + 1) * size, :] = free_im
    half = rows // 2
    f_re, f_im = frep[:half, :], frep[half:, :]
    d_re, d_im = drep[:half, :], drep[half:, :]
    total[:half, :] = d_re * f_re - d_im * f_im
    total[half:rows, :] = d_re * f_im + d_im * f_re

    free_sums = weighted_sums(mult, total[...])[:1]

    def take_sum(source, value):
        sum_copy(source, me).wait_recv()
        return value + lrecv[source][:, :rows]

    own_sums = lsend[me][:, :rows] + free_sums[:, :rows]
    ksend[...] = free_sums
    ksend[:, :rows] = lax.fori_loop(me + 1, n_hist, take_sum, own_sums)

    def local_copy(source, target):
        return pltpu.make_async_remote_copy(
            src_ref=ksend,
            dst_ref=krecv.at[source],
            send_sem=ksend_sem.at[target],
            recv_sem=krecv_sem.at[source],
            device_id={"ka": target},
            device_id_type=pl.DeviceIdType.MESH,
        )

    for hop in range(1, n_ka):
        local_copy(my_ka, lax.rem(my_ka + hop, n_ka)).start()
    local = ksend[...]
    for hop in range(1, n_ka):
        source = lax.rem(my_ka + hop, n_ka)
        local_copy(source, my_ka).wait_recv()
        local = local + krecv[source]
    local = jnp.broadcast_to(local / local[:, rows : rows + 1], (8, lanes))
    local_out[...] = local

    lane8 = lax.broadcasted_iota(jnp.int32, local.shape, 1)
    row8 = lax.broadcasted_iota(jnp.int32, local.shape, 0)

    def diagonal(s, a):
        lane = ((s * orb + a) * orb + a) * block + row8
        picked = jnp.where((lane8 == lane) & (row8 < block), local, 0.0)
        return jnp.sum(picked, axis=1, keepdims=True)[:block]

    self_re = jnp.zeros((block, 2 * states), jnp.float32)
    self_im = self_re
    for a in range(orb):
        h_re, h_im = diagonal(0, a), diagonal(1, a)
        r_re, r_im = reached[a]
        self_re += h_re * r_re - h_im * r_im
        self_im += h_re * r_im + h_im * r_re
    part = jnp.zeros((times, 2 * states), jnp.float32)
    for m in range(block):
        part += self_re[m : m + 1] * turned[m, 0] + self_im[m : m + 1] * turned[m, 1]
    for q in range(n_hist):
        qsend[q] = part[q * block : (q + 1) * block]

    def give_pseudo(target, carry):
        pseudo_copy(me, target).start()
        return carry

    lax.fori_loop(0, me, give_pseudo, 0)

    def take_part(source, value):
        part_copy(source, me).wait_recv()
        return value + precv[source].astype(jnp.float32)

    fresh = total[:rows, :] + psend[me].astype(jnp.float32)
    total_out[...] = lax.fori_loop(me + 1, n_hist, take_part, fresh)

    def take_pseudo(source, value):
        pseudo_copy(source, me).wait_recv()
        return value + qrecv[source]

    pseudo_out[...] = lax.fori_loop(me + 1, n_hist, take_pseudo, free_pseudo + qsend[me])

    def settle(target, carry):
        energy_copy(me, target).wait_send()
        sum_copy(me, target).wait_send()
        part_copy(me, target).wait_send()
        pseudo_copy(me, target).wait_send()
        return carry

    lax.fori_loop(0, me, settle, 0)
    for hop in range(1, n_ka):
        local_copy(my_ka, lax.rem(my_ka + hop, n_ka)).wait_send()


def lay_out(total_ref, local_ref, pseudo_ref, lattice_out, local_out, pseudo_out):
    block, orb = lattice_out.shape[:2]
    states = pseudo_out.shape[2]
    half = total_ref.shape[0] // 2
    for a in range(orb):
        for c in range(orb):
            row = (a * orb + c) * block
            for j in range(block):
                pair = total_ref[pl.ds(row + j, 2, stride=half), :]
                lattice_out[j, a, c] = pair.astype(jnp.bfloat16)
            for s in range(2):
                at = s * half + row
                local_out[a, c, s : s + 1, :] = local_ref[0:1, at : at + block]
    for p in range(2):
        pseudo_out[p] = pseudo_ref[:, p * states : (p + 1) * states]


def per_device(
    n_hist,
    n_ka,
    step_index,
    band_energy,
    kernel_row,
    lattice_history,
    diagonal_inverse,
    multiplicity,
    state_energy,
    connection,
    predicted_row,
    pseudo_history,
):
    block, orb, lanes = band_energy.shape
    times = lattice_history.shape[4]
    states = state_energy.shape[0]
    pairs = 2 * orb * orb
    rows = pairs * block
    per_tile = tile_rows // block
    vmem = pl.BlockSpec(memory_space=pltpu.VMEM)
    f32, bf16 = jnp.float32, jnp.bfloat16
    dma = pltpu.SemaphoreType.DMA
    operands = (
        jnp.transpose(band_energy, (1, 0, 2)),
        jnp.transpose(kernel_row, (0, 2, 3, 1, 4)),
        lattice_history,
        jnp.transpose(diagonal_inverse, (1, 2, 0, 3)),
        multiplicity[None],
        state_energy[None],
        jnp.transpose(connection),
        jnp.transpose(predicted_row, (0, 2, 1)),
        jnp.transpose(pseudo_history, (0, 1, 3, 2)),
    )
    results = pl.pallas_call(
        functools.partial(kernel, n_hist, n_ka),
        out_shape=(
            jax.ShapeDtypeStruct((rows, lanes), f32),
            jax.ShapeDtypeStruct((8, lanes), f32),
            jax.ShapeDtypeStruct((block, 2 * states), f32),
        ),
        in_specs=[pl.BlockSpec(memory_space=pltpu.SMEM)]
        + [pl.BlockSpec(memory_space=pl.ANY)] * len(operands),
        out_specs=(vmem, vmem, vmem),
        scratch_shapes=[
            *[pltpu.VMEM(array.shape, array.dtype) for array in operands],
            pltpu.VMEM((block, orb, orb, 2, lanes), f32),
            pltpu.VMEM((orb * block, lanes), f32),
            pltpu.VMEM((per_tile, rows, lanes), f32),
            pltpu.VMEM((8, lanes), f32),
            pltpu.VMEM((n_hist, 8, lanes), f32),
            pltpu.VMEM((n_hist, 1, lanes), f32),
            pltpu.VMEM((n_hist, 1, lanes), f32),
            pltpu.VMEM((n_hist, rows, lanes), bf16),
            pltpu.VMEM((n_hist, rows, lanes), bf16),
            pltpu.VMEM((rows, lanes), f32),
            pltpu.VMEM((rows, lanes), f32),
            pltpu.VMEM((lanes, lanes), f32),
            pltpu.VMEM((1, lanes), f32),
            pltpu.VMEM((n_ka, 1, lanes), f32),
            pltpu.VMEM((block, 2, times, 2 * states), f32),
            pltpu.VMEM((n_hist, block, 2 * states), f32),
            pltpu.VMEM((n_hist, block, 2 * states), f32),
            dma((len(operands),)),
            dma((n_hist,)),
            dma((n_hist,)),
            dma((n_hist,)),
            dma((n_hist,)),
            dma((n_hist,)),
            dma((n_hist,)),
            dma((n_ka,)),
            dma((n_ka,)),
            dma((n_hist,)),
            dma((n_hist,)),
        ],
        compiler_params=pltpu.CompilerParams(collective_id=0, has_side_effects=True),
    )(
        step_index,
        *operands,
    )
    lattice, local, pseudo = pl.pallas_call(
        lay_out,
        out_shape=(
            jax.ShapeDtypeStruct((block, orb, orb, 2, lanes), bf16),
            jax.ShapeDtypeStruct((orb, orb, 2, block), f32),
            jax.ShapeDtypeStruct((2, block, states), f32),
        ),
        in_specs=[vmem] * 3,
        out_specs=(vmem, vmem, vmem),
    )(*results)
    return (
        jnp.transpose(lattice, (0, 3, 1, 2, 4)),
        jnp.transpose(local, (2, 0, 1, 3)),
        jnp.transpose(pseudo, (0, 2, 1)),
    )


def solution(mesh):
    in_specs = (
        P(),
        P("hist", None, "ka"),
        P("hist", None, None, None, "ka"),
        P("hist", None, None, None, None, "ka"),
        P(None, None, None, "ka"),
        P("ka"),
        P(),
        P(),
        P(None, None, "hist"),
        P("hist", None, None, None),
    )
    out_specs = (
        P("hist", None, None, None, "ka"),
        P(None, None, None, "hist"),
        P(None, None, "hist"),
    )
    return jax.shard_map(
        functools.partial(per_device, mesh.shape["hist"], mesh.shape["ka"]),
        mesh=mesh,
        in_specs=in_specs,
        out_specs=out_specs,
        check_vma=False,
    )
```

```python
import functools

import jax
import jax.numpy as jnp
from jax import lax
from jax.experimental import pallas as pl
from jax.experimental.pallas import tpu as pltpu
from jax.sharding import PartitionSpec as P

time_step = 0.05
coupling = 0.02
tile_rows = 16
highest = lax.Precision.HIGHEST


def weighted_sums(mult, values):
    upper = values.astype(jnp.bfloat16)
    lower = (values - upper.astype(jnp.float32)).astype(jnp.bfloat16)
    return dot_rows(mult, upper) + dot_rows(mult, lower)


def dot_rows(left, right, precision=None):
    return lax.dot_general(
        left,
        right,
        (((1,), (1,)), ((), ())),
        precision=precision,
        preferred_element_type=jnp.float32,
    )


def kernel(
    n_hist,
    n_ka,
    step_ref,
    band_any,
    krow_any,
    hist_any,
    dinv_any,
    mult_any,
    energy_any,
    conn_any,
    pred_any,
    pseudo_any,
    total_out,
    local_out,
    pseudo_out,
    band_ref,
    krow_ref,
    hist_ref,
    dinv_ref,
    mult_ref,
    energy_ref,
    conn_ref,
    pred_ref,
    pseudo_ref,
    kw,
    suffix,
    stage,
    esend,
    erecv,
    lsend,
    lrecv,
    psend,
    precv,
    drep,
    frep,
    total,
    ksend,
    krecv,
    turned,
    qsend,
    qrecv,
    load_sem,
    esend_sem,
    erecv_sem,
    lsend_sem,
    lrecv_sem,
    psend_sem,
    precv_sem,
    ksend_sem,
    krecv_sem,
    qsend_sem,
    qrecv_sem,
):
    orb, block, lanes = band_ref.shape
    times = hist_ref.shape[4]
    states = energy_ref.shape[1]
    pairs = 2 * orb * orb
    rows = pairs * block
    per_tile = tile_rows // block
    me = lax.axis_index("hist")
    my_ka = lax.axis_index("ka")

    barrier = pltpu.get_barrier_semaphore()

    def greet(hop, carry):
        pl.semaphore_signal(
            barrier, inc=1, device_id={"hist": lax.rem(me + hop, n_hist)},
            device_id_type=pl.DeviceIdType.MESH,
        )
        return carry

    lax.fori_loop(1, n_hist, greet, 0)
    for hop in range(1, n_ka):
        pl.semaphore_signal(
            barrier, inc=1, device_id={"ka": lax.rem(my_ka + hop, n_ka)},
            device_id_type=pl.DeviceIdType.MESH,
        )

    sources = (
        krow_any, band_any, mult_any, hist_any, dinv_any, energy_any, conn_any, pred_any, pseudo_any
    )
    targets = (
        krow_ref, band_ref, mult_ref, hist_ref, dinv_ref, energy_ref, conn_ref, pred_ref, pseudo_ref
    )
    loads = [
        pltpu.make_async_copy(source, target, load_sem.at[i])
        for i, (source, target) in enumerate(zip(sources, targets))
    ]
    for load in loads:
        load.start()

    current = step_ref[0]
    first = me * block
    before = [jnp.where(first + m < current, 1.0, 0.0) for m in range(block)]
    weight = [
        jnp.where(first + m == 0, 0.5, 1.0) * before[m] for m in range(block)
    ]

    for load in loads[:3]:
        load.wait()
    for m in range(block):
        kw[m] = krow_ref[m].astype(jnp.float32) * weight[m]

    esend[...] = jnp.zeros(esend.shape, jnp.float32)
    for c in range(orb):
        run = jnp.zeros((1, lanes), jnp.float32)
        for m in reversed(range(block)):
            run = run + band_ref[c, m : m + 1, :] * before[m]
            suffix[c * block + m : c * block + m + 1, :] = run
        esend[c : c + 1, :] = run
    mult = jnp.broadcast_to(mult_ref[...].astype(jnp.float32), (8, lanes)).astype(jnp.bfloat16)

    pl.semaphore_wait(barrier, n_hist - 1 + n_ka - 1)

    def hist_copy(src, dst, send_sem, recv_sem, source, target):
        return pltpu.make_async_remote_copy(
            src_ref=src,
            dst_ref=dst.at[source],
            send_sem=send_sem.at[target],
            recv_sem=recv_sem.at[source],
            device_id={"hist": target},
            device_id_type=pl.DeviceIdType.MESH,
        )

    def energy_copy(source, target):
        return hist_copy(esend, erecv, esend_sem, erecv_sem, source, target)

    def sum_copy(source, target):
        return hist_copy(lsend.at[target], lrecv, lsend_sem, lrecv_sem, source, target)

    def part_copy(source, target):
        return hist_copy(psend.at[target], precv, psend_sem, precv_sem, source, target)

    def pseudo_copy(source, target):
        return hist_copy(qsend.at[target], qrecv, qsend_sem, qrecv_sem, source, target)

    def give_energy(target, carry):
        energy_copy(me, target).start()
        return carry

    lax.fori_loop(0, me, give_energy, 0)
    for load in loads[3:]:
        load.wait()

    def one_tile(tile, carry):
        at = pl.ds(pl.multiple_of(tile * tile_rows, tile_rows), tile_rows)
        zero = jnp.zeros((tile_rows, lanes), jnp.float32)
        real = [[zero] * orb for _ in range(orb)]
        imag = [[zero] * orb for _ in range(orb)]
        for m in range(block):
            for b in range(orb):
                k_re = [kw[m, a, b, 0:1, :] for a in range(orb)]
                k_im = [kw[m, a, b, 1:2, :] for a in range(orb)]
                for c in range(orb):
                    h_re = hist_ref[m, 0, b, c, at, :].astype(jnp.float32)
                    h_im = hist_ref[m, 1, b, c, at, :].astype(jnp.float32)
                    for a in range(orb):
                        real[a][c] += k_re[a] * h_re - k_im[a] * h_im
                        imag[a][c] += k_re[a] * h_im + k_im[a] * h_re
        for a in range(orb):
            for c in range(orb):
                out_re, out_im = zero, zero
                for b in range(orb):
                    d_re = dinv_ref[a, b, 0:1, :]
                    d_im = dinv_ref[a, b, 1:2, :]
                    out_re += d_re * real[b][c] - d_im * imag[b][c]
                    out_im += d_re * imag[b][c] + d_im * real[b][c]
                for s, value in enumerate((out_re, out_im)):
                    row = ((s * orb + a) * orb + c) * block
                    for d in range(per_tile):
                        stage[d, row : row + block, :] = value[d * block : (d + 1) * block]
        sums = weighted_sums(mult, stage[...].reshape(per_tile * rows, lanes))
        for d in range(per_tile):
            target = tile * per_tile + d
            lsend[target, :, :rows] = sums[:1, d * rows : (d + 1) * rows]

            @pl.when(target < me)
            def _():
                sum_copy(me, target).start()

        for d in range(per_tile):
            psend[tile * per_tile + d] = stage[d].astype(jnp.bfloat16)
        return carry

    lax.fori_loop(0, first // tile_rows + 1, one_tile, 0)

    def give_part(target, carry):
        part_copy(me, target).start()
        return carry

    lax.fori_loop(0, me, give_part, 0)

    for s in range(2):
        for a in range(orb):
            for c in range(orb):
                row = ((s * orb + a) * orb + c) * block
                drep[row : row + block, :] = jnp.broadcast_to(
                    dinv_ref[a, c, s : s + 1, :], (block, lanes)
                )
    total[rows:, :] = jnp.ones((lanes - rows, lanes), jnp.float32)
    def take_energy(source, later):
        energy_copy(source, me).wait_recv()
        return later + erecv[source]

    later = lax.fori_loop(
        me + 1, n_hist, take_energy, jnp.zeros(esend.shape, jnp.float32)
    )
    for c in range(orb):
        for j in range(block):
            frep[c * block + j : c * block + j + 1, :] = (
                later[c : c + 1] + suffix[c * block + j : c * block + j + 1, :]
            )
    size = orb * block
    angle = time_step * frep[:size, :]
    when = first + lax.rem(lax.broadcasted_iota(jnp.int32, (size, lanes), 0), block)
    inside = jnp.where(when <= current, 1.0, 0.0)
    free_re = -jnp.sin(angle) * inside
    free_im = -jnp.cos(angle) * inside
    for a in range(orb):
        frep[a * size : (a + 1) * size, :] = free_re
        frep[(orb + a) * size : (orb + a + 1) * size, :] = free_im
    half = rows // 2
    f_re, f_im = frep[:half, :], frep[half:, :]
    d_re, d_im = drep[:half, :], drep[half:, :]
    total[:half, :] = d_re * f_re - d_im * f_im
    total[half:rows, :] = d_re * f_im + d_im * f_re

    free_sums = weighted_sums(mult, total[...])[:1]

    def take_sum(source, value):
        sum_copy(source, me).wait_recv()
        return value + lrecv[source][:, :rows]

    own_sums = lsend[me][:, :rows] + free_sums[:, :rows]
    ksend[...] = free_sums
    ksend[:, :rows] = lax.fori_loop(me + 1, n_hist, take_sum, own_sums)

    def local_copy(source, target):
        return pltpu.make_async_remote_copy(
            src_ref=ksend,
            dst_ref=krecv.at[source],
            send_sem=ksend_sem.at[target],
            recv_sem=krecv_sem.at[source],
            device_id={"ka": target},
            device_id_type=pl.DeviceIdType.MESH,
        )

    for hop in range(1, n_ka):
        local_copy(my_ka, lax.rem(my_ka + hop, n_ka)).start()
    for m in range(block):
        h_re = pseudo_ref[m, 0].astype(jnp.float32)
        h_im = pseudo_ref[m, 1].astype(jnp.float32)
        turned[m, 0] = jnp.concatenate([h_re, h_im], axis=1)
        turned[m, 1] = jnp.concatenate([-h_im, h_re], axis=1)

    row_of = lax.broadcasted_iota(jnp.int32, (block, 2 * states), 0)
    lane_of = lax.broadcasted_iota(jnp.int32, (block, 2 * states), 1)
    row_time = first + row_of
    row_weight = jnp.where(row_time == 0, 0.5, 1.0) * jnp.where(row_time < current, 1.0, 0.0)
    conn = jnp.concatenate([conn_ref[...], conn_ref[...]], axis=1)
    reach = lax.broadcasted_iota(jnp.int32, (states, 2 * states), 0)
    reached = []
    for a in range(orb):
        hit = jnp.where(conn[2 * a : 2 * a + 1] == reach, 1.0, 0.0) + jnp.where(
            conn[2 * a + 1 : 2 * a + 2] == reach, 1.0, 0.0
        )
        reached.append(
            [
                jnp.dot(pred_ref[p], hit, precision=highest, preferred_element_type=jnp.float32)
                * row_weight
                * coupling
                for p in range(2)
            ]
        )
    energies = jnp.concatenate([energy_ref[...], energy_ref[...]], axis=1)
    spins = energies * time_step * (current - row_time).astype(jnp.float32)
    free_pseudo = jnp.where(lane_of < states, -jnp.sin(spins), -jnp.cos(spins))
    free_pseudo = free_pseudo * jnp.where(row_time <= current, 1.0, 0.0)

    local = ksend[...]
    for hop in range(1, n_ka):
        source = lax.rem(my_ka + hop, n_ka)
        local_copy(source, my_ka).wait_recv()
        local = local + krecv[source]
    local = jnp.broadcast_to(local / local[:, rows : rows + 1], (8, lanes))
    local_out[...] = local

    lane8 = lax.broadcasted_iota(jnp.int32, local.shape, 1)
    row8 = lax.broadcasted_iota(jnp.int32, local.shape, 0)

    def diagonal(s, a):
        lane = ((s * orb + a) * orb + a) * block + row8
        picked = jnp.where((lane8 == lane) & (row8 < block), local, 0.0)
        return jnp.sum(picked, axis=1, keepdims=True)[:block]

    self_re = jnp.zeros((block, 2 * states), jnp.float32)
    self_im = self_re
    for a in range(orb):
        h_re, h_im = diagonal(0, a), diagonal(1, a)
        r_re, r_im = reached[a]
        self_re += h_re * r_re - h_im * r_im
        self_im += h_re * r_im + h_im * r_re
    part = jnp.zeros((times, 2 * states), jnp.float32)
    for m in range(block):
        part += self_re[m : m + 1] * turned[m, 0] + self_im[m : m + 1] * turned[m, 1]
    for q in range(n_hist):
        qsend[q] = part[q * block : (q + 1) * block]

    def give_pseudo(target, carry):
        pseudo_copy(me, target).start()
        return carry

    lax.fori_loop(0, me, give_pseudo, 0)

    def take_part(source, value):
        part_copy(source, me).wait_recv()
        return value + precv[source].astype(jnp.float32)

    fresh = total[:rows, :] + psend[me].astype(jnp.float32)
    total_out[...] = lax.fori_loop(me + 1, n_hist, take_part, fresh)

    def take_pseudo(source, value):
        pseudo_copy(source, me).wait_recv()
        return value + qrecv[source]

    pseudo_out[...] = lax.fori_loop(me + 1, n_hist, take_pseudo, free_pseudo + qsend[me])

    def settle(target, carry):
        energy_copy(me, target).wait_send()
        sum_copy(me, target).wait_send()
        part_copy(me, target).wait_send()
        pseudo_copy(me, target).wait_send()
        return carry

    lax.fori_loop(0, me, settle, 0)
    for hop in range(1, n_ka):
        local_copy(my_ka, lax.rem(my_ka + hop, n_ka)).wait_send()


def lay_out(total_ref, local_ref, pseudo_ref, lattice_out, local_out, pseudo_out):
    block, orb = lattice_out.shape[:2]
    states = pseudo_out.shape[2]
    half = total_ref.shape[0] // 2
    for a in range(orb):
        for c in range(orb):
            row = (a * orb + c) * block
            for j in range(block):
                pair = total_ref[pl.ds(row + j, 2, stride=half), :]
                lattice_out[j, a, c] = pair.astype(jnp.bfloat16)
            for s in range(2):
                at = s * half + row
                local_out[a, c, s : s + 1, :] = local_ref[0:1, at : at + block]
    for p in range(2):
        pseudo_out[p] = pseudo_ref[:, p * states : (p + 1) * states]


def per_device(
    n_hist,
    n_ka,
    step_index,
    band_energy,
    kernel_row,
    lattice_history,
    diagonal_inverse,
    multiplicity,
    state_energy,
    connection,
    predicted_row,
    pseudo_history,
):
    block, orb, lanes = band_energy.shape
    times = lattice_history.shape[4]
    states = state_energy.shape[0]
    pairs = 2 * orb * orb
    rows = pairs * block
    per_tile = tile_rows // block
    vmem = pl.BlockSpec(memory_space=pltpu.VMEM)
    f32, bf16 = jnp.float32, jnp.bfloat16
    dma = pltpu.SemaphoreType.DMA
    operands = (
        jnp.transpose(band_energy, (1, 0, 2)),
        jnp.transpose(kernel_row, (0, 2, 3, 1, 4)),
        lattice_history,
        jnp.transpose(diagonal_inverse, (1, 2, 0, 3)),
        multiplicity[None],
        state_energy[None],
        jnp.transpose(connection),
        jnp.transpose(predicted_row, (0, 2, 1)),
        jnp.transpose(pseudo_history, (0, 1, 3, 2)),
    )
    results = pl.pallas_call(
        functools.partial(kernel, n_hist, n_ka),
        out_shape=(
            jax.ShapeDtypeStruct((rows, lanes), f32),
            jax.ShapeDtypeStruct((8, lanes), f32),
            jax.ShapeDtypeStruct((block, 2 * states), f32),
        ),
        in_specs=[pl.BlockSpec(memory_space=pltpu.SMEM)]
        + [pl.BlockSpec(memory_space=pl.ANY)] * len(operands),
        out_specs=(vmem, vmem, vmem),
        scratch_shapes=[
            *[pltpu.VMEM(array.shape, array.dtype) for array in operands],
            pltpu.VMEM((block, orb, orb, 2, lanes), f32),
            pltpu.VMEM((orb * block, lanes), f32),
            pltpu.VMEM((per_tile, rows, lanes), f32),
            pltpu.VMEM((8, lanes), f32),
            pltpu.VMEM((n_hist, 8, lanes), f32),
            pltpu.VMEM((n_hist, 1, lanes), f32),
            pltpu.VMEM((n_hist, 1, lanes), f32),
            pltpu.VMEM((n_hist, rows, lanes), bf16),
            pltpu.VMEM((n_hist, rows, lanes), bf16),
            pltpu.VMEM((rows, lanes), f32),
            pltpu.VMEM((rows, lanes), f32),
            pltpu.VMEM((lanes, lanes), f32),
            pltpu.VMEM((1, lanes), f32),
            pltpu.VMEM((n_ka, 1, lanes), f32),
            pltpu.VMEM((block, 2, times, 2 * states), f32),
            pltpu.VMEM((n_hist, block, 2 * states), f32),
            pltpu.VMEM((n_hist, block, 2 * states), f32),
            dma((len(operands),)),
            dma((n_hist,)),
            dma((n_hist,)),
            dma((n_hist,)),
            dma((n_hist,)),
            dma((n_hist,)),
            dma((n_hist,)),
            dma((n_ka,)),
            dma((n_ka,)),
            dma((n_hist,)),
            dma((n_hist,)),
        ],
        compiler_params=pltpu.CompilerParams(collective_id=0, has_side_effects=True),
    )(
        step_index,
        *operands,
    )
    lattice, local, pseudo = pl.pallas_call(
        lay_out,
        out_shape=(
            jax.ShapeDtypeStruct((block, orb, orb, 2, lanes), bf16),
            jax.ShapeDtypeStruct((orb, orb, 2, block), f32),
            jax.ShapeDtypeStruct((2, block, states), f32),
        ),
        in_specs=[vmem] * 3,
        out_specs=(vmem, vmem, vmem),
    )(*results)
    return (
        jnp.transpose(lattice, (0, 3, 1, 2, 4)),
        jnp.transpose(local, (2, 0, 1, 3)),
        jnp.transpose(pseudo, (0, 2, 1)),
    )


def solution(mesh):
    in_specs = (
        P(),
        P("hist", None, "ka"),
        P("hist", None, None, None, "ka"),
        P("hist", None, None, None, None, "ka"),
        P(None, None, None, "ka"),
        P("ka"),
        P(),
        P(),
        P(None, None, "hist"),
        P("hist", None, None, None),
    )
    out_specs = (
        P("hist", None, None, None, "ka"),
        P(None, None, None, "hist"),
        P(None, None, "hist"),
    )
    return jax.shard_map(
        functools.partial(per_device, mesh.shape["hist"], mesh.shape["ka"]),
        mesh=mesh,
        in_specs=in_specs,
        out_specs=out_specs,
        check_vma=False,
    )
```
